32 devices in a mesh: groups: 2 (over x), beam: 16 (over z, y, core).
Axes of the slice: x: 2, y: 2, z: 4, core: 2. Of those that a mesh axis runs over, the one named last changes fastest.
Arguments:
- transmission: float32 [2, 2, 512, 512], P('groups'), parts along dimension 0, may hold values from -1 to 1, as said below
- beams: int32 [16, 2], P('beam'), may hold values from -64 to 63
- phases: int32 [32, 16], replicated, may hold values from 0 to 63
- positions: int32 [32, 2], replicated, may hold values from 0 to 128
- owner: int32 [32], replicated, may hold values from 0 to 15, as said below
Outputs:
- patterns: float32 [128, 128, 128], P(('groups', 'beam')), parts along dimension 0
The draws below stay inside these ranges and needn't reach their ends.
There are 2 independent parts, one for each index of `groups`. The reference program is written for one: setup_inputs(seed, part) draws one part's arguments, and reference() takes and returns one part's arrays. A program takes and returns all parts, laid end to end along the dimension named above; an argument that names none is the same for every part. Nothing has to cross between parts.
Inputs may be any that keep to these rules, and one draw needn't show every extreme that they name: `transmission`: real and imaginary parts of each pixel form a pair of magnitude at most 1. Each owner is given at most 4 probes, and some owner exactly 4.
All inputs are finite; a program needn't handle non-finite values.
Results may differ from the reference program's by a relative error of at most 0.0003.
Values sent between devices are 32-bit elements; how exact they have to be, the bound alone decides.
No kernel may reach another device: no remote copies, remote signals or barrier semaphores. Data moves between devices by JAX's collectives and lax.ppermute only.
A program may use at most 64 MiB of HBM per device.

```python
import math
import jax
import jax.numpy as jnp
from jax import lax

GRID = 512
CROP = 256
WINDOW = 128
SLICES = 1
LEVELS = 64
BEAMS = 16
PROBES = 32
CAP = 4
SLOTS = 64


def draw_transmission(key, part):
    key_amp, key_angle = jax.random.split(key, 2)
    array_shape = (SLICES, GRID, GRID)
    magnitude = jax.random.uniform(key_amp, array_shape, jnp.float32, 0.6, 1.0)
    phase_angle = jax.random.uniform(key_angle, array_shape, jnp.float32, -math.pi, math.pi)
    return jnp.stack([magnitude * jnp.cos(phase_angle), magnitude * jnp.sin(phase_angle)], axis=1).astype(jnp.float32)


def draw_owner(key, part):
    key_perm, key_full, key_order = jax.random.split(key, 3)
    owners_total = SLOTS // CAP
    shuffled_slots = jax.random.permutation(key_perm, SLOTS)
    full_owner = jax.random.randint(key_full, (), 0, owners_total)
    priority = jnp.where(shuffled_slots // CAP == full_owner, 0, SLOTS) + jnp.arange(SLOTS)
    chosen = shuffled_slots[jnp.argsort(priority)][:PROBES]
    mixed = chosen[jax.random.permutation(key_order, PROBES)]
    return (mixed // CAP).astype(jnp.int32)


def with_ends(entries, own_key, smallest, top_value):
    index_at = [jax.random.randint(jax.random.fold_in(own_key, axis), (), 0, length) for axis, length in enumerate(entries.shape)]
    longest = entries.shape.index(max(entries.shape))
    beside = index_at[:longest] + [(index_at[longest] + 1) % entries.shape[longest]] + index_at[longest + 1:]
    return entries.at[tuple(index_at)].set(smallest).at[tuple(beside)].set(top_value)


def setup_inputs(seed: int = 0, part: int = 0) -> dict:
    arg_keys = jax.random.split(jax.random.key(seed), 6)
    part_keys = jax.random.split(jax.random.fold_in(arg_keys[5], part), 6)
    return {
        "transmission": draw_transmission(jax.random.fold_in(jax.random.fold_in(arg_keys[5], part), 71), part),
        "beams": with_ends(jax.random.randint(arg_keys[1], (BEAMS, 2), 0 - GRID // 8, GRID // 8), jax.random.fold_in(arg_keys[1], 1), 0 - GRID // 8, (GRID // 8) - 1).astype(jnp.int32),
        "phases": with_ends(jax.random.randint(arg_keys[2], (PROBES, BEAMS), 0, LEVELS), jax.random.fold_in(arg_keys[2], 1), 0, LEVELS - 1).astype(jnp.int32),
        "positions": with_ends(jax.random.randint(arg_keys[3], (PROBES, 2), 0, CROP - WINDOW + 1), jax.random.fold_in(arg_keys[3], 1), 0, CROP - WINDOW).astype(jnp.int32),
        "owner": draw_owner(jax.random.fold_in(arg_keys[5], 71), part),
    }


highest = lax.Precision.HIGHEST
prop_rate = 0.0004 * math.pi
two_pi = 2.0 * math.pi

def reference(transmission, beams, phases, positions, owner):
    index = jnp.arange(GRID, dtype=jnp.int32)
    signed = jnp.where(index < GRID // 2, index, index - GRID)
    prop_angle = (signed[:, None] * signed[:, None] + signed[None, :] * signed[None, :]).astype(jnp.float32) * prop_rate
    propagate = lax.complex(jnp.cos(prop_angle), -jnp.sin(prop_angle))
    lower = (GRID - CROP) // 2

    def one_beam(beam_pair):
        angles = ((beam_pair[0] * index[:, None] + beam_pair[1] * index[None, :]) % GRID).astype(jnp.float32) * (two_pi / GRID)
        wave = lax.complex(jnp.cos(angles), jnp.sin(angles))
        for slice_index in range(SLICES):
            specimen = lax.complex(transmission[slice_index, 0], transmission[slice_index, 1])
            wave = jnp.fft.ifft2(jnp.fft.fft2(specimen * wave) * propagate)
        cropped = wave[lower:lower + CROP, lower:lower + CROP]
        return jnp.stack([jnp.real(cropped), jnp.imag(cropped)])
    exits = lax.map(one_beam, beams)
    beam_total = beams.shape[0]
    weight_angle = phases.astype(jnp.float32) * (two_pi / LEVELS)
    weight_real = jnp.cos(weight_angle) / math.sqrt(beam_total)
    weight_imag = jnp.sin(weight_angle) / math.sqrt(beam_total)

    def one_probe(inputs):
        real_weight, imag_weight, offset = inputs
        window = lax.dynamic_slice(exits, (jnp.int32(0), jnp.int32(0), offset[0], offset[1]), (beam_total, 2, WINDOW, WINDOW))
        real_sum = jnp.einsum('b,byx->yx', real_weight, window[:, 0], precision=highest) - jnp.einsum('b,byx->yx', imag_weight, window[:, 1], precision=highest)
        imag_sum = jnp.einsum('b,byx->yx', real_weight, window[:, 1], precision=highest) + jnp.einsum('b,byx->yx', imag_weight, window[:, 0], precision=highest)
        spectrum = jnp.fft.fft2(lax.complex(real_sum, imag_sum))
        return (jnp.real(spectrum) * jnp.real(spectrum) + jnp.imag(spectrum) * jnp.imag(spectrum)) / (WINDOW * WINDOW)
    powers = lax.map(one_probe, (weight_real, weight_imag, positions))
    probe_ids = jnp.arange(PROBES, dtype=jnp.int32)
    same_owner = owner[:, None] == owner[None, :]
    earlier = probe_ids[None, :] < probe_ids[:, None]
    rank = lax.optimization_barrier(jnp.sum(jnp.where(same_owner & earlier, 1, 0), axis=1)).astype(jnp.int32)
    target = owner * CAP + rank
    return jnp.zeros((SLOTS, WINDOW, WINDOW), jnp.float32).at[target].set(powers.astype(jnp.float32))
```

```python
import math

import jax
import jax.numpy as jnp
import numpy as np
from jax import lax
from jax.experimental import pallas as pl
from jax.experimental.pallas import tpu as pltpu
from jax.sharding import PartitionSpec as P

CROP = 256
WINDOW = 128
LEVELS = 64
CAP = 4
SPAN = CROP - WINDOW

prop_rate = 0.0004 * math.pi
two_pi = 2.0 * math.pi


def window_operator(length):
    index = np.arange(length)
    freq = np.where(index < length // 2, index, index - length)
    kernel = np.fft.ifft(np.exp(-1j * prop_rate * freq.astype(np.float64) ** 2))
    lower = (length - CROP) // 2
    rows = np.arange(-SPAN, length + 8)
    point = np.arange(WINDOW)
    shifted = kernel[(lower + point[None, :] - rows[:, None]) % length]
    wave = np.exp(-1j * two_pi * (point[:, None] * point[None, :] % WINDOW) / WINDOW)
    table = shifted @ wave / math.sqrt(WINDOW)
    return np.concatenate([table.real, table.imag], axis=1).astype(np.float32)


def split(value):
    high = value.astype(jnp.bfloat16)
    return high, (value - high.astype(jnp.float32)).astype(jnp.bfloat16)


def dot(left, right):
    return jnp.dot(left, right, preferred_element_type=jnp.float32)


def moved(table_ref, start, length):
    whole = start // 8
    rows = table_ref[pl.ds(pl.multiple_of(whole * 8, 8), length + 8), :]
    return pltpu.roll(rows, length + 8 - (start - whole * 8), axis=0)[:length]


def place_kernel(offset_ref, table_ref, left_ref, right_ref):
    length = right_ref.shape[2]

    for slot in range(left_ref.shape[0]):
        rows = moved(table_ref, SPAN - offset_ref[slot, 0], length).T
        left_ref[slot, 0], left_ref[slot, 1] = split(rows)
        cols = moved(table_ref, SPAN - offset_ref[slot, 1], length)
        right_ref[slot, 0], right_ref[slot, 1] = split(cols)


def cosine(turns, length):
    quarter = length // 4
    shift = quarter.bit_length() - 1
    turns = turns & (length - 1)
    quadrant = (turns + quarter // 2) >> shift
    angle = (turns - (quadrant << shift)).astype(jnp.float32) * (two_pi / length)
    square = angle * angle
    even = 1.0 + square * (-1.0 / 2 + square * (1.0 / 24 + square * (-1.0 / 720 + square * (1.0 / 40320))))
    odd = angle * (1.0 + square * (-1.0 / 6 + square * (1.0 / 120 + square * (-1.0 / 5040))))
    value = jnp.where((quadrant & 1) == 0, even, odd)
    return jnp.where(((quadrant + 1) & 2) == 0, value, -value)


def probe_kernel(beam_ref, weight_ref, transmission_ref, left_ref, right_ref, out_ref, lit_ref):
    length = transmission_ref.shape[-1]
    beams = beam_ref.shape[0]
    depth = pl.cdiv(6 * beams, 128) * 128
    quarter = length // 4
    row_freq = beam_ref[:, 0:128]
    col_freq = beam_ref[:, 128:256]
    lane = lax.broadcasted_iota(jnp.int32, (beams, depth), 1)
    member = lax.broadcasted_iota(jnp.int32, (beams, depth), 0)
    wide = jnp.concatenate([row_freq] * (depth // 128), axis=1)
    freq = jnp.sum(jnp.where(lane % beams == member, wide, 0), axis=0, keepdims=True)
    block = lax.broadcasted_iota(jnp.int32, (1, depth), 1) // beams
    pixel = lax.broadcasted_iota(jnp.int32, (length, depth), 0)
    waves = cosine(pixel * freq - jnp.where(block % 2 == 1, quarter, 0), length)
    high, low = split(waves)
    high = high.astype(jnp.float32)
    low = low.astype(jnp.float32)
    rows = jnp.where(block < 4, high, jnp.where(block < 6, low, 0.0)).astype(jnp.bfloat16)
    pixel = lax.broadcasted_iota(jnp.int32, (beams, length), 1)
    turns = pixel * jnp.concatenate([col_freq] * (length // 128), axis=1)
    col_cos = cosine(turns, length)
    col_sin = cosine(turns - quarter, length)
    for slot in range(out_ref.shape[0]):
        weight_real = weight_ref[slot, 0]
        weight_imag = weight_ref[slot, 1]
        real = weight_real * col_cos - weight_imag * col_sin
        imag = weight_real * col_sin + weight_imag * col_cos
        for_cos = split(jnp.concatenate([real, imag], axis=1))
        for_sin = split(jnp.concatenate([-imag, real], axis=1))
        parts = [for_cos[0], for_sin[0], for_cos[1], for_sin[1], for_cos[0], for_sin[0]]
        if depth > 6 * beams:
            parts.append(jnp.zeros((depth - 6 * beams, 2 * length), jnp.bfloat16))
        lit = dot(rows, jnp.concatenate(parts, axis=0))
        light_real, light_imag = lit[:, :length], lit[:, length:]
        real, imag = transmission_ref[0, 0], transmission_ref[0, 1]
        lit_ref[0, 0:length], lit_ref[1, 0:length] = split(real * light_real - imag * light_imag)
        lit_ref[0, length:], lit_ref[1, length:] = split(real * light_imag + imag * light_real)
        source = jnp.concatenate([lit_ref[0], lit_ref[1], lit_ref[0]], axis=1)
        right = jnp.concatenate([right_ref[slot, 0], right_ref[slot, 0], right_ref[slot, 1]], axis=0)
        half = dot(source, right)
        high, low = split(
            jnp.concatenate(
                [
                    half[:length, :WINDOW] - half[length:, WINDOW:],
                    half[:length, WINDOW:] + half[length:, :WINDOW],
                ],
                axis=1,
            )
        )
        left = jnp.concatenate([left_ref[slot, 0], left_ref[slot, 0], left_ref[slot, 1]], axis=1)
        full = dot(left, jnp.concatenate([high, low, high], axis=0))
        real = full[:WINDOW, :WINDOW] - full[WINDOW:, WINDOW:]
        imag = full[:WINDOW, WINDOW:] + full[WINDOW:, :WINDOW]
        out_ref[slot] = real * real + imag * imag


def local(transmission, beams, phases, positions, owner):
    length = transmission.shape[-1]
    beam_count = lax.axis_size("beam")
    probes, beam_total = phases.shape
    sent = jnp.broadcast_to(beams[:, :, None], (beam_count, 2, 128)).reshape(beam_count, 256)
    every = lax.all_to_all(sent, "beam", split_axis=0, concat_axis=0, tiled=True)
    ids = jnp.arange(probes, dtype=jnp.int32)
    mine = owner == lax.axis_index("beam")
    rank = jnp.sum(jnp.where(mine[None, :] & (ids[None, :] < ids[:, None]), 1, 0), axis=1)
    chosen = mine[None, :] & (rank[None, :] == jnp.arange(CAP, dtype=jnp.int32)[:, None])
    offset = jnp.sum(jnp.where(chosen[:, :, None], positions[None], 0), axis=1)
    phase = jnp.sum(jnp.where(chosen[:, :, None], phases[None], 0), axis=1)
    angle = phase.astype(jnp.float32) * (two_pi / LEVELS)
    scale = jnp.where(jnp.any(chosen, axis=1), 1.0 / math.sqrt(beam_total), 0.0)[:, None]
    weight = jnp.stack([jnp.cos(angle) * scale, jnp.sin(angle) * scale], axis=1)[..., None]
    vmem = pl.BlockSpec(memory_space=pltpu.VMEM)
    left, right = pl.pallas_call(
        place_kernel,
        out_shape=(
            jax.ShapeDtypeStruct((CAP, 2, 2 * WINDOW, length), jnp.bfloat16),
            jax.ShapeDtypeStruct((CAP, 2, length, 2 * WINDOW), jnp.bfloat16),
        ),
        in_specs=[pl.BlockSpec(memory_space=pltpu.SMEM), vmem],
        out_specs=(vmem, vmem),
        name="place",
    )(offset, jnp.asarray(window_operator(length)))
    return pl.pallas_call(
        probe_kernel,
        out_shape=jax.ShapeDtypeStruct((CAP, WINDOW, WINDOW), jnp.float32),
        in_specs=[vmem] * 5,
        out_specs=vmem,
        scratch_shapes=[pltpu.VMEM((2, 2 * length, length), jnp.bfloat16)],
        name="probes",
    )(every, weight, transmission, left, right)


def solution(mesh):
    in_specs = (P("groups", None, None, None), P("beam", None), P(), P(), P())
    out_specs = P(("groups", "beam"), None, None)
    return jax.shard_map(local, mesh=mesh, in_specs=in_specs, out_specs=out_specs, check_vma=False)
```

```python
import math

import jax
import jax.numpy as jnp
import numpy as np
from jax import lax
from jax.experimental import pallas as pl
from jax.experimental.pallas import tpu as pltpu
from jax.sharding import PartitionSpec as P


CROP = 256
WINDOW = 128
LEVELS = 64
CAP = 4
SPAN = CROP - WINDOW
VMEM_LIMIT = 40 << 20
STEP = 32
WIDE = 256

prop_rate = 0.0004 * math.pi
two_pi = 2.0 * math.pi


def window_operator(length):
    index = np.arange(length)
    freq = np.where(index < length // 2, index, index - length)
    kernel = np.fft.ifft(np.exp(-1j * prop_rate * freq.astype(np.float64) ** 2))
    lower = (length - CROP) // 2
    rows = np.arange(-SPAN, length + 8)
    point = np.arange(WINDOW)
    shifted = kernel[(lower + point[None, :] - rows[:, None]) % length]
    wave = np.exp(-1j * two_pi * (point[:, None] * point[None, :] % WINDOW) / WINDOW)
    table = shifted @ wave / math.sqrt(WINDOW)
    return np.concatenate([table.real, table.imag], axis=1).astype(np.float32)


def row_operator(table):
    rows = table[SPAN : table.shape[0] - 8].T
    high = rows.astype(jnp.bfloat16)
    low = (rows - high.astype(np.float32)).astype(jnp.bfloat16)
    return np.concatenate([high, high, low], axis=1)


def partners(count):
    return [1 << bit | 1 for bit in range(1, count.bit_length() - 1)] + [1]


def split(value):
    high = value.astype(jnp.bfloat16)
    return high, (value - high.astype(jnp.float32)).astype(jnp.bfloat16)


def dot(left, right):
    return jnp.dot(left, right, preferred_element_type=jnp.float32)


def moved(table_ref, start, length):
    whole = start // 8
    rest = start - whole * 8
    width = table_ref.shape[1]
    rows = table_ref[pl.ds(pl.multiple_of(whole * 8, 8), length + 8), :].reshape(length // 8 + 1, 8, width)
    rows = pltpu.roll(rows, jnp.where(rest == 0, 0, 8 - rest), axis=1)
    inside = lax.broadcasted_iota(jnp.int32, (1, 8, width), 1) < 8 - rest
    return jnp.where(inside, rows[:-1], rows[1:]).reshape(length, width)


def pick_kernel(owner_hbm, position_hbm, phase_hbm, weight_ref, offset_ref, owner_ref, position_ref, phase_ref, pick_ref, sems):
    slots, (beams, probes) = weight_ref.shape[0], phase_ref.shape
    pairs = [(owner_hbm, owner_ref), (position_hbm, position_ref), (phase_hbm, phase_ref)]
    copies = [pltpu.make_async_copy(*pair, sems.at[index]) for index, pair in enumerate(pairs)]
    for copy in copies:
        copy.start()
    me = lax.axis_index("beam")
    for slot in range(slots):
        pick_ref[slot] = -1
    lane = lax.broadcasted_iota(jnp.int32, (beams, probes), 1)
    row = lax.broadcasted_iota(jnp.int32, (beams, 128), 0)
    column = lax.broadcasted_iota(jnp.int32, (beams, 128), 1)
    flips = jnp.zeros_like(column)
    for step, mask in enumerate(partners(beams)):
        flips = flips ^ jnp.where((column >> step & 1) == 1, mask, 0)
    copies[0].wait()

    def visit(probe, count):
        hit = owner_ref[probe] == me
        pick_ref[jnp.where(hit, count, slots)] = probe
        return count + jnp.where(hit, 1, 0)

    lax.fori_loop(0, probes, visit, 0)
    for copy in copies[1:]:
        copy.wait()
    for slot in range(slots):
        pick = pick_ref[slot]
        level = jnp.sum(jnp.where(lane == pick, phase_ref[...], 0), axis=1, keepdims=True)
        level = jnp.sum(jnp.where(row == flips ^ me, level, 0), axis=0, keepdims=True)
        level = jnp.sum(jnp.where(row == column, level, 0), axis=1, keepdims=True)
        level = jnp.broadcast_to(level, (beams, 128))
        scale = jnp.where(pick >= 0, 1.0 / math.sqrt(beams), 0.0)
        weight_ref[slot, 0] = cosine(level, LEVELS) * scale
        weight_ref[slot, 1] = cosine(level - LEVELS // 4, LEVELS) * scale
        probe = jnp.maximum(pick, 0)
        offset_ref[2 * slot] = position_ref[0, probe]
        offset_ref[2 * slot + 1] = position_ref[1, probe]


def fetch_kernel(specimen_hbm, specimen_ref, sem):
    copy = pltpu.make_async_copy(specimen_hbm.at[0, :, :, 0 : specimen_ref.shape[2]], specimen_ref, sem)
    copy.start()
    copy.wait()


def place_kernel(offset_hbm, table_hbm, right_ref, offset_ref, table_ref, sems):
    slots, length = right_ref.shape[0], right_ref.shape[2]
    copies = [
        pltpu.make_async_copy(table_hbm, table_ref, sems.at[0]),
        pltpu.make_async_copy(offset_hbm, offset_ref, sems.at[1]),
    ]
    for copy in copies:
        copy.start()
    for copy in copies:
        copy.wait()
    for slot in range(slots):
        cols = moved(table_ref, SPAN - offset_ref[2 * slot + 1], length)
        right_ref[slot, 0], right_ref[slot, 1] = split(cols)


def cosine(turns, length):
    quarter = length // 4
    shift = quarter.bit_length() - 1
    turns = turns & (length - 1)
    quadrant = (turns + quarter // 2) >> shift
    angle = (turns - (quadrant << shift)).astype(jnp.float32) * (two_pi / length)
    square = angle * angle
    even = 1.0 + square * (-1.0 / 2 + square * (1.0 / 24 + square * (-1.0 / 720 + square * (1.0 / 40320))))
    odd = angle * (1.0 + square * (-1.0 / 6 + square * (1.0 / 120 + square * (-1.0 / 5040))))
    value = jnp.where((quadrant & 1) == 0, even, odd)
    return jnp.where(((quadrant + 1) & 2) == 0, value, -value)


def probe_kernel(
    beam_ref,
    weight_ref,
    near_ref,
    right_ref,
    offset_ref,
    transmission_hbm,
    left_hbm,
    out_hbm,
    far_ref,
    left_ref,
    row_ref,
    col_ref,
    mix_ref,
    light_ref,
    lit_ref,
    half_ref,
    out_ref,
    start_ref,
    sems,
    out_sems,
):
    slots, length = out_ref.shape[0], transmission_hbm.shape[-1]
    beams = beam_ref.shape[0]
    depth = row_ref.shape[1]
    quarter = length // 4
    copy = pltpu.make_async_copy(offset_ref, start_ref, sems.at[0])
    copy.start()
    far = pltpu.make_async_copy(transmission_hbm.at[0, :, :, length // 2 :], far_ref, sems.at[2])
    far.start()
    left = pltpu.make_async_copy(left_hbm, left_ref, sems.at[1])
    left.start()
    row_freq = beam_ref[:, 0, 0:128]
    col_freq = beam_ref[:, 0, 128:256]
    lane = lax.broadcasted_iota(jnp.int32, (beams, depth), 1)
    member = lax.broadcasted_iota(jnp.int32, (beams, depth), 0)
    wide = jnp.concatenate([row_freq] * (depth // 128), axis=1)
    freq = jnp.sum(jnp.where(lane % beams == member, wide, 0), axis=0, keepdims=True)
    block = lax.broadcasted_iota(jnp.int32, (1, depth), 1) // beams
    shift = jnp.where(block % 2 == 1, quarter, 0)
    fine = lax.broadcasted_iota(jnp.int32, (STEP, depth), 0) * freq
    fine_cos, fine_sin = cosine(fine, length), cosine(fine - quarter, length)
    coarse = lax.broadcasted_iota(jnp.int32, (length // STEP, depth), 0) * (STEP * freq) - shift
    coarse_cos, coarse_sin = cosine(coarse, length), cosine(coarse - quarter, length)
    for index in range(length // STEP):
        waves = coarse_cos[index : index + 1] * fine_cos - coarse_sin[index : index + 1] * fine_sin
        high = waves.astype(jnp.bfloat16).astype(jnp.float32)
        parts = jnp.where(block < 4, high, jnp.where(block < 6, waves - high, 0.0))
        row_ref[index * STEP : (index + 1) * STEP] = parts.astype(jnp.bfloat16)
    pixel = lax.broadcasted_iota(jnp.int32, (beams, length), 1)
    turns = pixel * jnp.concatenate([col_freq] * (length // 128), axis=1)
    col_ref[0] = cosine(turns, length)
    col_ref[1] = cosine(turns - quarter, length)
    if depth > 6 * beams:
        for way in range(mix_ref.shape[0]):
            mix_ref[way, 6 * beams :] = jnp.zeros((depth - 6 * beams, 2 * length), jnp.bfloat16)

    def light(slot, way):
        weight_real = jnp.concatenate([weight_ref[slot, 0]] * (length // 128), axis=1)
        weight_imag = jnp.concatenate([weight_ref[slot, 1]] * (length // 128), axis=1)
        real = weight_real * col_ref[0] - weight_imag * col_ref[1]
        imag = weight_real * col_ref[1] + weight_imag * col_ref[0]
        tiles = [slice(start, start + 128) for start in range(0, length, 128)]
        for_cos = split(jnp.concatenate([x[:, tile] for tile in tiles for x in (real, imag)], axis=1))
        for_sin = split(jnp.concatenate([x[:, tile] for tile in tiles for x in (-imag, real)], axis=1))
        parts = [for_cos[0], for_sin[0], for_cos[1], for_sin[1], for_cos[0], for_sin[0]]
        for index, part in enumerate(parts):
            mix_ref[way, index * beams : (index + 1) * beams] = part

    def light_tile(tile, way):
        light_ref[way, tile] = dot(row_ref[...], mix_ref[way, :, tile * 256 : (tile + 1) * 256])

    def shine(tile, way):
        specimen_ref = near_ref if tile * 128 < length // 2 else far_ref
        cols = slice(tile * 128 % (length // 2), tile * 128 % (length // 2) + 128)
        stretch, start = tile * 128 // WIDE, tile * 128 % WIDE
        lanes = slice(start, start + 128)
        for row in range(0, length, 32):
            rows = slice(row, row + 32)
            light_real, light_imag = light_ref[way, tile, rows, 0:128], light_ref[way, tile, rows, 128:256]
            real, imag = specimen_ref[0, rows, cols], specimen_ref[1, rows, cols]
            high, low = split(real * light_real - imag * light_imag)
            lit_ref[way, stretch, 0, rows, lanes], lit_ref[way, stretch, 1, rows, lanes] = high, low
            high, low = split(real * light_imag + imag * light_real)
            lit_ref[way, length // WIDE + stretch, 0, rows, lanes], lit_ref[way, length // WIDE + stretch, 1, rows, lanes] = high, low

    def along_cols(slot, way):
        source, operator = [], []
        for stretch in range(2 * length // WIDE):
            rows = slice(stretch * WIDE % length, stretch * WIDE % length + WIDE)
            high, low = right_ref[slot, 0, rows], right_ref[slot, 1, rows]
            if stretch * WIDE >= length:
                high, low = (jnp.concatenate([-x[:, WINDOW:], x[:, :WINDOW]], axis=1) for x in (high, low))
            source += [lit_ref[way, stretch, 0], lit_ref[way, stretch, 0], lit_ref[way, stretch, 1]]
            operator += [high, low, high]
        half = dot(jnp.concatenate(source, axis=1), jnp.concatenate(operator, axis=0))
        half_ref[way, 0:length] = half
        half_ref[way, length:] = half[0 : SPAN + 8]

    def along_rows(slot, way):
        high, low = split(moved(half_ref.at[way], start_ref[2 * slot], length))
        full = dot(left_ref[...], jnp.concatenate([high, low, high], axis=0))
        real = full[:WINDOW, :WINDOW] - full[WINDOW:, WINDOW:]
        imag = full[:WINDOW, WINDOW:] + full[WINDOW:, :WINDOW]
        out_ref[slot] = real * real + imag * imag
        pltpu.make_async_copy(out_ref.at[slot], out_hbm.at[slot], out_sems.at[slot]).start()

    def prepare(slot):
        light(slot, slot)
        light_tile(0, slot)
        for tile in range(1, length // 128):
            light_tile(tile, slot)
            if slot == 0 and tile == length // 256 + 1:
                far.wait()
            shine(tile - 1, slot)
        shine(length // 128 - 1, slot)

    prepare(0)
    for slot in range(slots):
        along_cols(slot, slot)
        if slot + 1 < slots:
            prepare(slot + 1)
    copy.wait()
    left.wait()
    for slot in range(slots):
        along_rows(slot, slot)
    for slot in range(slots):
        pltpu.make_async_copy(out_ref.at[slot], out_hbm.at[slot], out_sems.at[slot]).wait()


def probe_call(every, weight, specimen, right, offset, transmission, left):
    length = transmission.shape[-1]
    depth = pl.cdiv(6 * every.shape[0], 128) * 128
    weight, specimen, right = (pltpu.with_memory_space_constraint(x, pltpu.VMEM) for x in (weight, specimen, right))
    transmission, left = (pltpu.with_memory_space_constraint(x, pltpu.HBM) for x in (transmission, left))
    vmem = pl.BlockSpec(memory_space=pltpu.VMEM)
    anywhere = pl.BlockSpec(memory_space=pltpu.HBM)
    return pl.pallas_call(
        probe_kernel,
        out_shape=jax.ShapeDtypeStruct((CAP, WINDOW, WINDOW), jnp.float32),
        in_specs=[vmem] * 4 + [pl.BlockSpec(memory_space=pl.ANY)] + [anywhere] * 2,
        out_specs=anywhere,
        scratch_shapes=[
            pltpu.VMEM(specimen.shape, specimen.dtype),
            pltpu.VMEM(left.shape, left.dtype),
            pltpu.VMEM((length, depth), jnp.bfloat16),
            pltpu.VMEM((2, every.shape[0], length), jnp.float32),
            pltpu.VMEM((CAP, depth, 2 * length), jnp.bfloat16),
            pltpu.VMEM((CAP, length // 128, length, 256), jnp.float32),
            pltpu.VMEM((CAP, 2 * length // WIDE, 2, length, WIDE), jnp.bfloat16),
            pltpu.VMEM((CAP, length + SPAN + 8, 2 * WINDOW), jnp.float32),
            pltpu.VMEM((CAP, WINDOW, WINDOW), jnp.float32),
            pltpu.SMEM((2 * CAP,), jnp.int32),
            pltpu.SemaphoreType.DMA((3,)),
            pltpu.SemaphoreType.DMA((CAP,)),
        ],
        compiler_params=pltpu.CompilerParams(vmem_limit_bytes=VMEM_LIMIT),
        name="probes",
    )(every, weight, specimen, right, offset, transmission, left)


def local(transmission, beams, phases, positions, owner):
    length = transmission.shape[-1]
    beam_count = lax.axis_size("beam")
    beam_total = phases.shape[1]
    every = jnp.broadcast_to(beams[:, :, None], (1, 2, 128)).reshape(1, 1, 256)
    for mask in partners(beam_count):
        pairs = [(here, here ^ mask) for here in range(beam_count)]
        other = lax.ppermute(every, "beam", pairs)
        every = jnp.concatenate([every, other], axis=0)
    vmem = pl.BlockSpec(memory_space=pltpu.VMEM)
    smem = pl.BlockSpec(memory_space=pltpu.SMEM)
    anywhere = pl.BlockSpec(memory_space=pltpu.HBM)
    params = pltpu.CompilerParams(vmem_limit_bytes=VMEM_LIMIT)
    weight, offset = pl.pallas_call(
        pick_kernel,
        out_shape=(
            pltpu.VMEM((CAP, 2, beam_total, 128), jnp.float32),
            jax.ShapeDtypeStruct((2 * CAP,), jnp.int32),
        ),
        in_specs=[anywhere] * 3,
        out_specs=(vmem, smem),
        scratch_shapes=[
            pltpu.SMEM(owner.shape, jnp.int32),
            pltpu.SMEM(positions.shape[::-1], jnp.int32),
            pltpu.VMEM(phases.shape[::-1], jnp.int32),
            pltpu.SMEM((CAP + 1,), jnp.int32),
            pltpu.SemaphoreType.DMA((3,)),
        ],
        compiler_params=params,
        name="pick",
    )(*(pltpu.with_memory_space_constraint(x, pltpu.HBM) for x in (owner, positions.T, phases.T)))
    specimen = pl.pallas_call(
        fetch_kernel,
        out_shape=pltpu.VMEM((2, length, length // 2), jnp.float32),
        in_specs=[anywhere],
        out_specs=vmem,
        scratch_shapes=[pltpu.SemaphoreType.DMA],
        compiler_params=params,
        name="fetch",
    )(pltpu.with_memory_space_constraint(transmission, pltpu.HBM))
    table = window_operator(length)
    right = pl.pallas_call(
        place_kernel,
        out_shape=pltpu.VMEM((CAP, 2, length, 2 * WINDOW), jnp.bfloat16),
        in_specs=[pl.BlockSpec(memory_space=pl.ANY), anywhere],
        out_specs=vmem,
        scratch_shapes=[
            pltpu.SMEM((2 * CAP,), jnp.int32),
            pltpu.VMEM(table.shape, jnp.float32),
            pltpu.SemaphoreType.DMA((2,)),
        ],
        compiler_params=params,
        name="place",
    )(offset, pltpu.with_memory_space_constraint(jnp.asarray(table), pltpu.HBM))
    return probe_call(every, weight, specimen, right, offset, transmission, jnp.asarray(row_operator(table)))


def solution(mesh):
    in_specs = (P("groups", None, None, None), P("beam", None), P(), P(), P())
    out_specs = P(("groups", "beam"), None, None)
    return jax.shard_map(local, mesh=mesh, in_specs=in_specs, out_specs=out_specs, check_vma=False)
```

```python
import math

import jax
import jax.numpy as jnp
import numpy as np
from jax import lax
from jax.experimental import pallas as pl
from jax.experimental.pallas import tpu as pltpu
from jax.sharding import PartitionSpec as P


CROP = 256
WINDOW = 128
LEVELS = 64
CAP = 4
SPAN = CROP - WINDOW
VMEM_LIMIT = 40 << 20
STEP = 32
WIDE = 256

prop_rate = 0.0004 * math.pi
two_pi = 2.0 * math.pi


def window_operator(length):
    index = np.arange(length)
    freq = np.where(index < length // 2, index, index - length)
    kernel = np.fft.ifft(np.exp(-1j * prop_rate * freq.astype(np.float64) ** 2))
    lower = (length - CROP) // 2
    rows = np.arange(-SPAN, length + 8)
    point = np.arange(WINDOW)
    shifted = kernel[(lower + point[None, :] - rows[:, None]) % length]
    wave = np.exp(-1j * two_pi * (point[:, None] * point[None, :] % WINDOW) / WINDOW)
    table = shifted @ wave / math.sqrt(WINDOW)
    return np.concatenate([table.real, table.imag], axis=1).astype(np.float32)


def row_operator(table):
    rows = table[SPAN : table.shape[0] - 8].T
    high = rows.astype(jnp.bfloat16)
    low = (rows - high.astype(np.float32)).astype(jnp.bfloat16)
    return np.concatenate([high, high, low], axis=1)


def partners(count):
    return [1 << bit | 1 for bit in range(1, count.bit_length() - 1)] + [1]


def split(value):
    high = value.astype(jnp.bfloat16)
    return high, (value - high.astype(jnp.float32)).astype(jnp.bfloat16)


def dot(left, right):
    return jnp.dot(left, right, preferred_element_type=jnp.float32)


def moved(table_ref, start, length):
    whole = start // 8
    rest = start - whole * 8
    width = table_ref.shape[1]
    rows = table_ref[pl.ds(pl.multiple_of(whole * 8, 8), length + 8), :].reshape(length // 8 + 1, 8, width)
    rows = pltpu.roll(rows, jnp.where(rest == 0, 0, 8 - rest), axis=1)
    inside = lax.broadcasted_iota(jnp.int32, (1, 8, width), 1) < 8 - rest
    return jnp.where(inside, rows[:-1], rows[1:]).reshape(length, width)


def pick_kernel(owner_hbm, position_hbm, pick_ref, owner_ref, position_ref, slot_ref, sems):
    slots, probes = pick_ref.shape[0] // 3, owner_ref.shape[0]
    pairs = [(owner_hbm, owner_ref), (position_hbm, position_ref)]
    copies = [pltpu.make_async_copy(*pair, sems.at[index]) for index, pair in enumerate(pairs)]
    for copy in copies:
        copy.start()
    me = lax.axis_index("beam")
    for slot in range(slots):
        slot_ref[slot] = -1
    copies[0].wait()

    def visit(probe, count):
        hit = owner_ref[probe] == me
        slot_ref[jnp.where(hit, count, slots)] = probe
        return count + jnp.where(hit, 1, 0)

    lax.fori_loop(0, probes, visit, 0, unroll=math.gcd(probes, 32))
    copies[1].wait()
    for slot in range(slots):
        probe = jnp.maximum(slot_ref[slot], 0)
        pick_ref[3 * slot] = slot_ref[slot]
        pick_ref[3 * slot + 1] = position_ref[0, probe]
        pick_ref[3 * slot + 2] = position_ref[1, probe]


def fetch_kernel(specimen_hbm, specimen_ref, sem):
    copy = pltpu.make_async_copy(specimen_hbm.at[0, :, :, 0 : specimen_ref.shape[2]], specimen_ref, sem)
    copy.start()
    copy.wait()


def place_kernel(pick_hbm, phase_hbm, table_hbm, weight_ref, right_ref, pick_ref, phase_ref, table_ref, sems):
    slots, length = right_ref.shape[0], right_ref.shape[2]
    beams, probes = phase_ref.shape
    half = length // 2
    cut = half + SPAN + 8
    pairs = [
        (pick_hbm, pick_ref),
        (phase_hbm, phase_ref),
        (table_hbm.at[0:cut], table_ref.at[0:cut]),
        (table_hbm.at[cut:], table_ref.at[cut:]),
    ]
    copies = [pltpu.make_async_copy(*pair, sems.at[index]) for index, pair in enumerate(pairs)]
    for copy in copies:
        copy.start()
    me = lax.axis_index("beam")
    lane = lax.broadcasted_iota(jnp.int32, (beams, probes), 1)
    row = lax.broadcasted_iota(jnp.int32, (beams, 128), 0)
    column = lax.broadcasted_iota(jnp.int32, (beams, 128), 1)
    flips = jnp.zeros_like(column)
    for step, mask in enumerate(partners(beams)):
        flips = flips ^ jnp.where((column >> step & 1) == 1, mask, 0)
    copies[0].wait()
    copies[1].wait()
    for slot in range(slots):
        pick = pick_ref[3 * slot]
        level = jnp.sum(jnp.where(lane == pick, phase_ref[...], 0), axis=1, keepdims=True)
        level = jnp.sum(jnp.where(row == flips ^ me, level, 0), axis=0, keepdims=True)
        level = jnp.sum(jnp.where(row == column, level, 0), axis=1, keepdims=True)
        level = jnp.broadcast_to(level, (beams, 128))
        scale = jnp.where(pick >= 0, 1.0 / math.sqrt(beams), 0.0)
        weight_ref[slot, 0] = cosine(level, LEVELS) * scale
        weight_ref[slot, 1] = cosine(level - LEVELS // 4, LEVELS) * scale
    for part in range(2):
        copies[2 + part].wait()
        rows = slice(part * half, (part + 1) * half)
        for slot in range(slots):
            cols = moved(table_ref, part * half + SPAN - pick_ref[3 * slot + 2], half)
            right_ref[slot, 0, rows], right_ref[slot, 1, rows] = split(cols)


def cosine(turns, length):
    quarter = length // 4
    shift = quarter.bit_length() - 1
    turns = turns & (length - 1)
    quadrant = (turns + quarter // 2) >> shift
    angle = (turns - (quadrant << shift)).astype(jnp.float32) * (two_pi / length)
    square = angle * angle
    even = 1.0 + square * (-1.0 / 2 + square * (1.0 / 24 + square * (-1.0 / 720 + square * (1.0 / 40320))))
    odd = angle * (1.0 + square * (-1.0 / 6 + square * (1.0 / 120 + square * (-1.0 / 5040))))
    value = jnp.where((quadrant & 1) == 0, even, odd)
    return jnp.where(((quadrant + 1) & 2) == 0, value, -value)


def probe_kernel(
    beam_ref,
    weight_ref,
    near_ref,
    right_ref,
    offset_ref,
    transmission_hbm,
    left_hbm,
    out_hbm,
    far_ref,
    left_ref,
    row_ref,
    col_ref,
    mix_ref,
    light_ref,
    lit_ref,
    half_refs,
    out_ref,
    start_ref,
    sems,
    out_sems,
):
    slots, length = out_ref.shape[0], transmission_hbm.shape[-1]
    beams = beam_ref.shape[0]
    depth = row_ref.shape[1]
    quarter = length // 4
    copy = pltpu.make_async_copy(offset_ref, start_ref, sems.at[0])
    copy.start()
    far = pltpu.make_async_copy(transmission_hbm.at[0, :, :, length // 2 :], far_ref, sems.at[2])
    far.start()
    left = pltpu.make_async_copy(left_hbm, left_ref, sems.at[1])
    left.start()
    row_freq = beam_ref[:, 0, 0:128]
    col_freq = beam_ref[:, 0, 128:256]
    lane = lax.broadcasted_iota(jnp.int32, (beams, depth), 1)
    member = lax.broadcasted_iota(jnp.int32, (beams, depth), 0)
    wide = jnp.concatenate([row_freq] * (depth // 128), axis=1)
    freq = jnp.sum(jnp.where(lane % beams == member, wide, 0), axis=0, keepdims=True)
    block = lax.broadcasted_iota(jnp.int32, (1, depth), 1) // beams
    shift = jnp.where(block % 2 == 1, quarter, 0)
    fine = lax.broadcasted_iota(jnp.int32, (STEP, depth), 0) * freq
    fine_cos, fine_sin = cosine(fine, length), cosine(fine - quarter, length)
    coarse = lax.broadcasted_iota(jnp.int32, (length // STEP, depth), 0) * (STEP * freq) - shift
    coarse_cos, coarse_sin = cosine(coarse, length), cosine(coarse - quarter, length)
    for index in range(length // STEP):
        waves = coarse_cos[index : index + 1] * fine_cos - coarse_sin[index : index + 1] * fine_sin
        high = waves.astype(jnp.bfloat16).astype(jnp.float32)
        parts = jnp.where(block < 4, high, jnp.where(block < 6, waves - high, 0.0))
        row_ref[index * STEP : (index + 1) * STEP] = parts.astype(jnp.bfloat16)
    pixel = lax.broadcasted_iota(jnp.int32, (beams, length), 1)
    turns = pixel * jnp.concatenate([col_freq] * (length // 128), axis=1)
    col_ref[0] = cosine(turns, length)
    col_ref[1] = cosine(turns - quarter, length)
    if depth > 6 * beams:
        for way in range(mix_ref.shape[0]):
            mix_ref[way, 6 * beams :] = jnp.zeros((depth - 6 * beams, 2 * length), jnp.bfloat16)

    def light(slot, way):
        weight_real = jnp.concatenate([weight_ref[slot, 0]] * (length // 128), axis=1)
        weight_imag = jnp.concatenate([weight_ref[slot, 1]] * (length // 128), axis=1)
        real = weight_real * col_ref[0] - weight_imag * col_ref[1]
        imag = weight_real * col_ref[1] + weight_imag * col_ref[0]
        tiles = [slice(start, start + 128) for start in range(0, length, 128)]
        for_cos = split(jnp.concatenate([x[:, tile] for tile in tiles for x in (real, imag)], axis=1))
        for_sin = split(jnp.concatenate([x[:, tile] for tile in tiles for x in (-imag, real)], axis=1))
        parts = [for_cos[0], for_sin[0], for_cos[1], for_sin[1], for_cos[0], for_sin[0]]
        for index, part in enumerate(parts):
            mix_ref[way, index * beams : (index + 1) * beams] = part

    def light_tile(tile, way):
        light_ref[way, tile] = dot(row_ref[...], mix_ref[way, :, tile * 256 : (tile + 1) * 256])

    def shine(tile, way):
        specimen_ref = near_ref if tile * 128 < length // 2 else far_ref
        cols = slice(tile * 128 % (length // 2), tile * 128 % (length // 2) + 128)
        stretch, start = tile * 128 // WIDE, tile * 128 % WIDE
        lanes = slice(start, start + 128)
        for row in range(0, length, 32):
            rows = slice(row, row + 32)
            light_real, light_imag = light_ref[way, tile, rows, 0:128], light_ref[way, tile, rows, 128:256]
            real, imag = specimen_ref[0, rows, cols], specimen_ref[1, rows, cols]
            high, low = split(real * light_real - imag * light_imag)
            lit_ref[way, stretch, 0, rows, lanes], lit_ref[way, stretch, 1, rows, lanes] = high, low
            high, low = split(real * light_imag + imag * light_real)
            lit_ref[way, length // WIDE + stretch, 0, rows, lanes], lit_ref[way, length // WIDE + stretch, 1, rows, lanes] = high, low

    def along_cols(slot, way):
        source, operator = [], []
        for stretch in range(2 * length // WIDE):
            rows = slice(stretch * WIDE % length, stretch * WIDE % length + WIDE)
            high, low = right_ref[slot, 0, rows], right_ref[slot, 1, rows]
            if stretch * WIDE >= length:
                high, low = (jnp.concatenate([-x[:, WINDOW:], x[:, :WINDOW]], axis=1) for x in (high, low))
            source += [lit_ref[way, stretch, 0], lit_ref[way, stretch, 0], lit_ref[way, stretch, 1]]
            operator += [high, low, high]
        half = dot(jnp.concatenate(source, axis=1), jnp.concatenate(operator, axis=0))
        half_refs[way][0:length] = half
        half_refs[way][length:] = half[0 : SPAN + 8]

    def along_rows(slot, way):
        high, low = split(moved(half_refs[way], start_ref[3 * slot + 1], length))
        full = dot(left_ref[...], jnp.concatenate([high, low, high], axis=0))
        real = full[:WINDOW, :WINDOW] - full[WINDOW:, WINDOW:]
        imag = full[:WINDOW, WINDOW:] + full[WINDOW:, :WINDOW]
        out_ref[slot] = real * real + imag * imag

    def prepare(slot):
        light(slot, slot)
        light_tile(0, slot)
        for tile in range(1, length // 128):
            light_tile(tile, slot)
            if slot == 0 and tile == length // 256 + 1:
                far.wait()
            shine(tile - 1, slot)
        shine(length // 128 - 1, slot)

    def send(slot):
        pltpu.make_async_copy(out_ref.at[slot], out_hbm.at[slot], out_sems.at[slot]).start()

    prepare(0)
    for slot in range(slots):
        if slot + 1 < slots:
            prepare(slot + 1)
        along_cols(slot, slot)
    copy.wait()
    left.wait()
    for slot in range(slots):
        along_rows(slot, slot)
    for slot in range(slots):
        send(slot)
    for slot in range(slots):
        pltpu.make_async_copy(out_ref.at[slot], out_hbm.at[slot], out_sems.at[slot]).wait()


def probe_call(every, weight, specimen, right, offset, transmission, left):
    length = transmission.shape[-1]
    depth = pl.cdiv(6 * every.shape[0], 128) * 128
    weight, specimen, right = (pltpu.with_memory_space_constraint(x, pltpu.VMEM) for x in (weight, specimen, right))
    transmission, left = (pltpu.with_memory_space_constraint(x, pltpu.HBM) for x in (transmission, left))
    vmem = pl.BlockSpec(memory_space=pltpu.VMEM)
    anywhere = pl.BlockSpec(memory_space=pltpu.HBM)
    return pl.pallas_call(
        probe_kernel,
        out_shape=jax.ShapeDtypeStruct((CAP, WINDOW, WINDOW), jnp.float32),
        in_specs=[vmem] * 4 + [pl.BlockSpec(memory_space=pl.ANY)] + [anywhere] * 2,
        out_specs=anywhere,
        scratch_shapes=[
            pltpu.VMEM(specimen.shape, specimen.dtype),
            pltpu.VMEM(left.shape, left.dtype),
            pltpu.VMEM((length, depth), jnp.bfloat16),
            pltpu.VMEM((2, every.shape[0], length), jnp.float32),
            pltpu.VMEM((CAP, depth, 2 * length), jnp.bfloat16),
            pltpu.VMEM((CAP, length // 128, length, 256), jnp.float32),
            pltpu.VMEM((CAP, 2 * length // WIDE, 2, length, WIDE), jnp.bfloat16),
            [pltpu.VMEM((length + SPAN + 8, 2 * WINDOW), jnp.float32) for _ in range(CAP)],
            pltpu.VMEM((CAP, WINDOW, WINDOW), jnp.float32),
            pltpu.SMEM((3 * CAP,), jnp.int32),
            pltpu.SemaphoreType.DMA((3,)),
            pltpu.SemaphoreType.DMA((CAP,)),
        ],
        compiler_params=pltpu.CompilerParams(vmem_limit_bytes=VMEM_LIMIT),
        name="probes",
    )(every, weight, specimen, right, offset, transmission, left)


def local(transmission, beams, phases, positions, owner):
    length = transmission.shape[-1]
    beam_count = lax.axis_size("beam")
    beam_total = phases.shape[1]
    every = jnp.broadcast_to(beams[:, :, None], (1, 2, 128)).reshape(1, 1, 256)
    for mask in partners(beam_count):
        pairs = [(here, here ^ mask) for here in range(beam_count)]
        other = lax.ppermute(every, "beam", pairs)
        every = jnp.concatenate([every, other], axis=0)
    vmem = pl.BlockSpec(memory_space=pltpu.VMEM)
    smem = pl.BlockSpec(memory_space=pltpu.SMEM)
    anywhere = pl.BlockSpec(memory_space=pltpu.HBM)
    params = pltpu.CompilerParams(vmem_limit_bytes=VMEM_LIMIT)
    pick = pl.pallas_call(
        pick_kernel,
        out_shape=jax.ShapeDtypeStruct((3 * CAP,), jnp.int32),
        in_specs=[anywhere] * 2,
        out_specs=smem,
        scratch_shapes=[
            pltpu.SMEM(owner.shape, jnp.int32),
            pltpu.SMEM(positions.shape[::-1], jnp.int32),
            pltpu.SMEM((CAP + 1,), jnp.int32),
            pltpu.SemaphoreType.DMA((2,)),
        ],
        compiler_params=params,
        name="pick",
    )(*(pltpu.with_memory_space_constraint(x, pltpu.HBM) for x in (owner, positions.T)))
    specimen = pl.pallas_call(
        fetch_kernel,
        out_shape=pltpu.VMEM((2, length, length // 2), jnp.float32),
        in_specs=[anywhere],
        out_specs=vmem,
        scratch_shapes=[pltpu.SemaphoreType.DMA],
        compiler_params=params,
        name="fetch",
    )(pltpu.with_memory_space_constraint(transmission, pltpu.HBM))
    table = window_operator(length)
    weight, right = pl.pallas_call(
        place_kernel,
        out_shape=(
            pltpu.VMEM((CAP, 2, beam_total, 128), jnp.float32),
            pltpu.VMEM((CAP, 2, length, 2 * WINDOW), jnp.bfloat16),
        ),
        in_specs=[pl.BlockSpec(memory_space=pl.ANY), anywhere, anywhere],
        out_specs=(vmem, vmem),
        scratch_shapes=[
            pltpu.SMEM((3 * CAP,), jnp.int32),
            pltpu.VMEM(phases.shape[::-1], jnp.int32),
            pltpu.VMEM(table.shape, jnp.float32),
            pltpu.SemaphoreType.DMA((4,)),
        ],
        compiler_params=params,
        name="place",
    )(pick, *(pltpu.with_memory_space_constraint(x, pltpu.HBM) for x in (phases.T, jnp.asarray(table))))
    return probe_call(every, weight, specimen, right, pick, transmission, jnp.asarray(row_operator(table)))


def solution(mesh):
    in_specs = (P("groups", None, None, None), P("beam", None), P(), P(), P())
    out_specs = P(("groups", "beam"), None, None)
    return jax.shard_map(local, mesh=mesh, in_specs=in_specs, out_specs=out_specs, check_vma=False)
```

```python
import math

import jax
import jax.numpy as jnp
import numpy as np
from jax import lax
from jax.experimental import pallas as pl
from jax.experimental.pallas import tpu as pltpu
from jax.sharding import PartitionSpec as P


CROP = 256
WINDOW = 128
LEVELS = 64
CAP = 4
SPAN = CROP - WINDOW
VMEM_LIMIT = 40 << 20
STEP = 32
WIDE = 256

prop_rate = 0.0004 * math.pi
two_pi = 2.0 * math.pi


def window_operator(length):
    index = np.arange(length)
    freq = np.where(index < length // 2, index, index - length)
    kernel = np.fft.ifft(np.exp(-1j * prop_rate * freq.astype(np.float64) ** 2))
    lower = (length - CROP) // 2
    rows = np.arange(-SPAN, length + 8)
    point = np.arange(WINDOW)
    shifted = kernel[(lower + point[None, :] - rows[:, None]) % length]
    wave = np.exp(-1j * two_pi * (point[:, None] * point[None, :] % WINDOW) / WINDOW)
    table = shifted @ wave / math.sqrt(WINDOW)
    return np.concatenate([table.real, table.imag], axis=1).astype(np.float32)


def row_operator(table):
    rows = table[SPAN : table.shape[0] - 8].T
    high = rows.astype(jnp.bfloat16)
    low = (rows - high.astype(np.float32)).astype(jnp.bfloat16)
    return np.concatenate([high, high, low], axis=1)


def partners(count):
    return [1 << bit | 1 for bit in range(count.bit_length() - 2, 0, -1)] + [1]


def split(value):
    high = value.astype(jnp.bfloat16)
    return high, (value - high.astype(jnp.float32)).astype(jnp.bfloat16)


def dot(left, right):
    return jnp.dot(left, right, preferred_element_type=jnp.float32)


def moved(table_ref, start, length):
    whole = start // 8
    rest = start - whole * 8
    width = table_ref.shape[1]
    rows = table_ref[pl.ds(pl.multiple_of(whole * 8, 8), length + 8), :].reshape(length // 8 + 1, 8, width)
    rows = pltpu.roll(rows, jnp.where(rest == 0, 0, 8 - rest), axis=1)
    inside = lax.broadcasted_iota(jnp.int32, (1, 8, width), 1) < 8 - rest
    return jnp.where(inside, rows[:-1], rows[1:]).reshape(length, width)


def pick_kernel(owner_hbm, position_hbm, pick_ref, owner_ref, position_ref, slot_ref, sems):
    slots, probes = pick_ref.shape[0] // 3, owner_ref.shape[0]
    pairs = [(owner_hbm, owner_ref), (position_hbm, position_ref)]
    copies = [pltpu.make_async_copy(*pair, sems.at[index]) for index, pair in enumerate(pairs)]
    for copy in copies:
        copy.start()
    me = lax.axis_index("beam")
    for slot in range(slots):
        slot_ref[slot] = -1
    copies[0].wait()

    def visit(probe, count):
        hit = owner_ref[probe] == me
        slot_ref[jnp.where(hit, count, slots)] = probe
        return count + jnp.where(hit, 1, 0)

    lax.fori_loop(0, probes, visit, 0, unroll=math.gcd(probes, 32))
    copies[1].wait()
    for slot in range(slots):
        probe = jnp.maximum(slot_ref[slot], 0)
        pick_ref[3 * slot] = slot_ref[slot]
        pick_ref[3 * slot + 1] = position_ref[0, probe]
        pick_ref[3 * slot + 2] = position_ref[1, probe]


def fetch_kernel(specimen_hbm, specimen_ref, sem):
    copy = pltpu.make_async_copy(specimen_hbm.at[0, :, :, 0 : specimen_ref.shape[2]], specimen_ref, sem)
    copy.start()
    copy.wait()


def place_kernel(pick_hbm, phase_hbm, table_hbm, weight_ref, right_ref, pick_ref, phase_ref, table_ref, sems):
    slots, length = right_ref.shape[0], right_ref.shape[2]
    beams, probes = phase_ref.shape
    half = length // 2
    cut = half + SPAN + 8
    pairs = [
        (pick_hbm, pick_ref),
        (phase_hbm, phase_ref),
        (table_hbm.at[0:cut], table_ref.at[0:cut]),
        (table_hbm.at[cut:], table_ref.at[cut:]),
    ]
    copies = [pltpu.make_async_copy(*pair, sems.at[index]) for index, pair in enumerate(pairs)]
    for copy in copies:
        copy.start()
    me = lax.axis_index("beam")
    lane = lax.broadcasted_iota(jnp.int32, (beams, probes), 1)
    row = lax.broadcasted_iota(jnp.int32, (beams, 128), 0)
    column = lax.broadcasted_iota(jnp.int32, (beams, 128), 1)
    flips = jnp.zeros_like(column)
    for step, mask in enumerate(partners(beams)):
        flips = flips ^ jnp.where((column >> step & 1) == 1, mask, 0)
    copies[0].wait()
    copies[1].wait()
    for slot in range(slots):
        pick = pick_ref[3 * slot]
        level = jnp.sum(jnp.where(lane == pick, phase_ref[...], 0), axis=1, keepdims=True)
        level = jnp.sum(jnp.where(row == flips ^ me, level, 0), axis=0, keepdims=True)
        level = jnp.sum(jnp.where(row == column, level, 0), axis=1, keepdims=True)
        level = jnp.broadcast_to(level, (beams, 128))
        scale = jnp.where(pick >= 0, 1.0 / math.sqrt(beams), 0.0)
        weight_ref[slot, 0] = cosine(level, LEVELS) * scale
        weight_ref[slot, 1] = cosine(level - LEVELS // 4, LEVELS) * scale
    for part in range(2):
        copies[2 + part].wait()
        rows = slice(part * half, (part + 1) * half)
        for slot in range(slots):
            cols = moved(table_ref, part * half + SPAN - pick_ref[3 * slot + 2], half)
            right_ref[slot, 0, rows], right_ref[slot, 1, rows] = split(cols)


def cosine(turns, length):
    quarter = length // 4
    shift = quarter.bit_length() - 1
    turns = turns & (length - 1)
    quadrant = (turns + quarter // 2) >> shift
    angle = (turns - (quadrant << shift)).astype(jnp.float32) * (two_pi / length)
    square = angle * angle
    even = 1.0 + square * (-1.0 / 2 + square * (1.0 / 24 + square * (-1.0 / 720 + square * (1.0 / 40320))))
    odd = angle * (1.0 + square * (-1.0 / 6 + square * (1.0 / 120 + square * (-1.0 / 5040))))
    value = jnp.where((quadrant & 1) == 0, even, odd)
    return jnp.where(((quadrant + 1) & 2) == 0, value, -value)


def probe_kernel(
    beam_ref,
    weight_ref,
    near_ref,
    right_ref,
    offset_ref,
    transmission_hbm,
    left_hbm,
    out_hbm,
    far_ref,
    left_ref,
    row_ref,
    col_ref,
    mix_ref,
    light_ref,
    lit_ref,
    half_refs,
    out_ref,
    start_ref,
    sems,
    out_sems,
):
    slots, length = out_ref.shape[0], transmission_hbm.shape[-1]
    beams = beam_ref.shape[0]
    depth = row_ref.shape[1]
    quarter = length // 4
    copy = pltpu.make_async_copy(offset_ref, start_ref, sems.at[0])
    copy.start()
    far = pltpu.make_async_copy(transmission_hbm.at[0, :, :, length // 2 :], far_ref, sems.at[2])
    far.start()
    left = pltpu.make_async_copy(left_hbm, left_ref, sems.at[1])
    left.start()
    row_freq = beam_ref[:, 0, 0:128]
    col_freq = beam_ref[:, 0, 128:256]
    lane = lax.broadcasted_iota(jnp.int32, (beams, depth), 1)
    member = lax.broadcasted_iota(jnp.int32, (beams, depth), 0)
    wide = jnp.concatenate([row_freq] * (depth // 128), axis=1)
    freq = jnp.sum(jnp.where(lane % beams == member, wide, 0), axis=0, keepdims=True)
    block = lax.broadcasted_iota(jnp.int32, (1, depth), 1) // beams
    shift = jnp.where(block % 2 == 1, quarter, 0)
    fine = lax.broadcasted_iota(jnp.int32, (STEP, depth), 0) * freq
    fine_cos, fine_sin = cosine(fine, length), cosine(fine - quarter, length)
    coarse = lax.broadcasted_iota(jnp.int32, (length // STEP, depth), 0) * (STEP * freq) - shift
    coarse_cos, coarse_sin = cosine(coarse, length), cosine(coarse - quarter, length)
    for index in range(length // STEP):
        waves = coarse_cos[index : index + 1] * fine_cos - coarse_sin[index : index + 1] * fine_sin
        high = waves.astype(jnp.bfloat16).astype(jnp.float32)
        parts = jnp.where(block < 4, high, jnp.where(block < 6, waves - high, 0.0))
        row_ref[index * STEP : (index + 1) * STEP] = parts.astype(jnp.bfloat16)
    pixel = lax.broadcasted_iota(jnp.int32, (beams, length), 1)
    turns = pixel * jnp.concatenate([col_freq] * (length // 128), axis=1)
    col_ref[0] = cosine(turns, length)
    col_ref[1] = cosine(turns - quarter, length)
    if depth > 6 * beams:
        for way in range(mix_ref.shape[0]):
            mix_ref[way, 6 * beams :] = jnp.zeros((depth - 6 * beams, 2 * length), jnp.bfloat16)

    def light(slot, way):
        weight_real = jnp.concatenate([weight_ref[slot, 0]] * (length // 128), axis=1)
        weight_imag = jnp.concatenate([weight_ref[slot, 1]] * (length // 128), axis=1)
        real = weight_real * col_ref[0] - weight_imag * col_ref[1]
        imag = weight_real * col_ref[1] + weight_imag * col_ref[0]
        tiles = [slice(start, start + 128) for start in range(0, length, 128)]
        for_cos = split(jnp.concatenate([x[:, tile] for tile in tiles for x in (real, imag)], axis=1))
        for_sin = split(jnp.concatenate([x[:, tile] for tile in tiles for x in (-imag, real)], axis=1))
        parts = [for_cos[0], for_sin[0], for_cos[1], for_sin[1], for_cos[0], for_sin[0]]
        for index, part in enumerate(parts):
            mix_ref[way, index * beams : (index + 1) * beams] = part

    def light_tile(tile, way):
        light_ref[way, tile] = dot(row_ref[...], mix_ref[way, :, tile * 256 : (tile + 1) * 256])

    def shine(tile, way):
        specimen_ref = near_ref if tile * 128 < length // 2 else far_ref
        cols = slice(tile * 128 % (length // 2), tile * 128 % (length // 2) + 128)
        stretch, start = tile * 128 // WIDE, tile * 128 % WIDE
        lanes = slice(start, start + 128)
        for row in range(0, length, 32):
            rows = slice(row, row + 32)
            light_real, light_imag = light_ref[way, tile, rows, 0:128], light_ref[way, tile, rows, 128:256]
            real, imag = specimen_ref[0, rows, cols], specimen_ref[1, rows, cols]
            high, low = split(real * light_real - imag * light_imag)
            lit_ref[way, stretch, 0, rows, lanes], lit_ref[way, stretch, 1, rows, lanes] = high, low
            high, low = split(real * light_imag + imag * light_real)
            lit_ref[way, length // WIDE + stretch, 0, rows, lanes], lit_ref[way, length // WIDE + stretch, 1, rows, lanes] = high, low

    def along_cols(slot, way):
        source, operator = [], []
        for stretch in range(2 * length // WIDE):
            rows = slice(stretch * WIDE % length, stretch * WIDE % length + WIDE)
            high, low = right_ref[slot, 0, rows], right_ref[slot, 1, rows]
            if stretch * WIDE >= length:
                high, low = (jnp.concatenate([-x[:, WINDOW:], x[:, :WINDOW]], axis=1) for x in (high, low))
            source += [lit_ref[way, stretch, 0], lit_ref[way, stretch, 0], lit_ref[way, stretch, 1]]
            operator += [high, low, high]
        half = dot(jnp.concatenate(source, axis=1), jnp.concatenate(operator, axis=0))
        half_refs[way][0:length] = half
        half_refs[way][length:] = half[0 : SPAN + 8]

    def along_rows(slot, way):
        high, low = split(moved(half_refs[way], start_ref[3 * slot + 1], length))
        full = dot(left_ref[...], jnp.concatenate([high, low, high], axis=0))
        real = full[:WINDOW, :WINDOW] - full[WINDOW:, WINDOW:]
        imag = full[:WINDOW, WINDOW:] + full[WINDOW:, :WINDOW]
        out_ref[slot] = real * real + imag * imag

    def prepare(slot):
        light(slot, slot)
        light_tile(0, slot)
        for tile in range(1, length // 128):
            light_tile(tile, slot)
            if slot == 0 and tile == length // 256 + 1:
                far.wait()
            shine(tile - 1, slot)
        shine(length // 128 - 1, slot)

    def send(slot):
        pltpu.make_async_copy(out_ref.at[slot], out_hbm.at[slot], out_sems.at[slot]).start()

    def run(count):
        ready = 0
        for slot in range(count):
            wanted = min(slot + 2 if count == slots or slot else 1, count)
            for coming in range(ready, wanted):
                prepare(coming)
            ready = wanted
            along_cols(slot, slot)
        left.wait()
        for slot in range(count):
            along_rows(slot, slot)
        for slot in range(count, slots):
            out_ref[slot] = jnp.zeros((WINDOW, WINDOW), jnp.float32)

    copy.wait()
    full = start_ref[3 * slots - 3] >= 0
    pl.when(full)(lambda: run(slots))
    pl.when(jnp.logical_not(full))(lambda: run(slots - 1))
    for slot in range(slots):
        send(slot)
    for slot in range(slots):
        pltpu.make_async_copy(out_ref.at[slot], out_hbm.at[slot], out_sems.at[slot]).wait()


def probe_call(every, weight, specimen, right, offset, transmission, left):
    length = transmission.shape[-1]
    depth = pl.cdiv(6 * every.shape[0], 128) * 128
    weight, specimen, right = (pltpu.with_memory_space_constraint(x, pltpu.VMEM) for x in (weight, specimen, right))
    transmission, left = (pltpu.with_memory_space_constraint(x, pltpu.HBM) for x in (transmission, left))
    vmem = pl.BlockSpec(memory_space=pltpu.VMEM)
    anywhere = pl.BlockSpec(memory_space=pltpu.HBM)
    return pl.pallas_call(
        probe_kernel,
        out_shape=jax.ShapeDtypeStruct((CAP, WINDOW, WINDOW), jnp.float32),
        in_specs=[vmem] * 4 + [pl.BlockSpec(memory_space=pl.ANY)] + [anywhere] * 2,
        out_specs=anywhere,
        scratch_shapes=[
            pltpu.VMEM(specimen.shape, specimen.dtype),
            pltpu.VMEM(left.shape, left.dtype),
            pltpu.VMEM((length, depth), jnp.bfloat16),
            pltpu.VMEM((2, every.shape[0], length), jnp.float32),
            pltpu.VMEM((CAP, depth, 2 * length), jnp.bfloat16),
            pltpu.VMEM((CAP, length // 128, length, 256), jnp.float32),
            pltpu.VMEM((CAP, 2 * length // WIDE, 2, length, WIDE), jnp.bfloat16),
            [pltpu.VMEM((length + SPAN + 8, 2 * WINDOW), jnp.float32) for _ in range(CAP)],
            pltpu.VMEM((CAP, WINDOW, WINDOW), jnp.float32),
            pltpu.SMEM((3 * CAP,), jnp.int32),
            pltpu.SemaphoreType.DMA((3,)),
            pltpu.SemaphoreType.DMA((CAP,)),
        ],
        compiler_params=pltpu.CompilerParams(vmem_limit_bytes=VMEM_LIMIT),
        name="probes",
    )(every, weight, specimen, right, offset, transmission, left)


def local(transmission, beams, phases, positions, owner):
    length = transmission.shape[-1]
    beam_count = lax.axis_size("beam")
    beam_total = phases.shape[1]
    every = jnp.broadcast_to(beams[:, :, None], (1, 2, 128)).reshape(1, 1, 256)
    for mask in partners(beam_count):
        pairs = [(here, here ^ mask) for here in range(beam_count)]
        other = lax.ppermute(every, "beam", pairs)
        every = jnp.concatenate([every, other], axis=0)
    vmem = pl.BlockSpec(memory_space=pltpu.VMEM)
    smem = pl.BlockSpec(memory_space=pltpu.SMEM)
    anywhere = pl.BlockSpec(memory_space=pltpu.HBM)
    params = pltpu.CompilerParams(vmem_limit_bytes=VMEM_LIMIT)
    pick = pl.pallas_call(
        pick_kernel,
        out_shape=jax.ShapeDtypeStruct((3 * CAP,), jnp.int32),
        in_specs=[anywhere] * 2,
        out_specs=smem,
        scratch_shapes=[
            pltpu.SMEM(owner.shape, jnp.int32),
            pltpu.SMEM(positions.shape[::-1], jnp.int32),
            pltpu.SMEM((CAP + 1,), jnp.int32),
            pltpu.SemaphoreType.DMA((2,)),
        ],
        compiler_params=params,
        name="pick",
    )(*(pltpu.with_memory_space_constraint(x, pltpu.HBM) for x in (owner, positions.T)))
    specimen = pl.pallas_call(
        fetch_kernel,
        out_shape=pltpu.VMEM((2, length, length // 2), jnp.float32),
        in_specs=[anywhere],
        out_specs=vmem,
        scratch_shapes=[pltpu.SemaphoreType.DMA],
        compiler_params=params,
        name="fetch",
    )(pltpu.with_memory_space_constraint(transmission, pltpu.HBM))
    table = window_operator(length)
    weight, right = pl.pallas_call(
        place_kernel,
        out_shape=(
            pltpu.VMEM((CAP, 2, beam_total, 128), jnp.float32),
            pltpu.VMEM((CAP, 2, length, 2 * WINDOW), jnp.bfloat16),
        ),
        in_specs=[pl.BlockSpec(memory_space=pl.ANY), anywhere, anywhere],
        out_specs=(vmem, vmem),
        scratch_shapes=[
            pltpu.SMEM((3 * CAP,), jnp.int32),
            pltpu.VMEM(phases.shape[::-1], jnp.int32),
            pltpu.VMEM(table.shape, jnp.float32),
            pltpu.SemaphoreType.DMA((4,)),
        ],
        compiler_params=params,
        name="place",
    )(pick, *(pltpu.with_memory_space_constraint(x, pltpu.HBM) for x in (phases.T, jnp.asarray(table))))
    return probe_call(every, weight, specimen, right, pick, transmission, jnp.asarray(row_operator(table)))


def solution(mesh):
    in_specs = (P("groups", None, None, None), P("beam", None), P(), P(), P())
    out_specs = P(("groups", "beam"), None, None)
    return jax.shard_map(local, mesh=mesh, in_specs=in_specs, out_specs=out_specs, check_vma=False)
```

```python
import math

import jax
import jax.numpy as jnp
import numpy as np
from jax import lax
from jax.experimental import pallas as pl
from jax.experimental.pallas import tpu as pltpu
from jax.sharding import PartitionSpec as P


CROP = 256
WINDOW = 128
LEVELS = 64
CAP = 4
SPAN = CROP - WINDOW
VMEM_LIMIT = 40 << 20
STEP = 32
WIDE = 256

prop_rate = 0.0004 * math.pi
two_pi = 2.0 * math.pi


def window_operator(length):
    index = np.arange(length)
    freq = np.where(index < length // 2, index, index - length)
    kernel = np.fft.ifft(np.exp(-1j * prop_rate * freq.astype(np.float64) ** 2))
    lower = (length - CROP) // 2
    rows = np.arange(-SPAN, length + 8)
    point = np.arange(WINDOW)
    shifted = kernel[(lower + point[None, :] - rows[:, None]) % length]
    wave = np.exp(-1j * two_pi * (point[:, None] * point[None, :] % WINDOW) / WINDOW)
    table = shifted @ wave / math.sqrt(WINDOW)
    return np.concatenate([table.real, table.imag], axis=1).astype(np.float32)


def row_operator(table):
    rows = table[SPAN : table.shape[0] - 8].T
    high = rows.astype(jnp.bfloat16)
    low = (rows - high.astype(np.float32)).astype(jnp.bfloat16)
    return np.concatenate([high, high, low], axis=1)


def partners(count):
    return [1 << bit | 1 for bit in range(count.bit_length() - 2, 0, -1)] + [1]


def split(value):
    high = value.astype(jnp.bfloat16)
    return high, (value - high.astype(jnp.float32)).astype(jnp.bfloat16)


def dot(left, right):
    return jnp.dot(left, right, preferred_element_type=jnp.float32)


def moved(table_ref, start, length):
    whole = start // 8
    rest = start - whole * 8
    width = table_ref.shape[1]
    rows = table_ref[pl.ds(pl.multiple_of(whole * 8, 8), length + 8), :].reshape(length // 8 + 1, 8, width)
    rows = pltpu.roll(rows, jnp.where(rest == 0, 0, 8 - rest), axis=1)
    inside = lax.broadcasted_iota(jnp.int32, (1, 8, width), 1) < 8 - rest
    return jnp.where(inside, rows[:-1], rows[1:]).reshape(length, width)


def pick_kernel(owner_hbm, position_hbm, pick_ref, owner_ref, position_ref, slot_ref, sems):
    slots, probes = pick_ref.shape[0] // 3, owner_ref.shape[0]
    pairs = [(owner_hbm, owner_ref), (position_hbm, position_ref)]
    copies = [pltpu.make_async_copy(*pair, sems.at[index]) for index, pair in enumerate(pairs)]
    for copy in copies:
        copy.start()
    me = lax.axis_index("beam")
    for slot in range(slots):
        slot_ref[slot] = -1
    copies[0].wait()

    def visit(probe, count):
        hit = owner_ref[probe] == me
        slot_ref[jnp.where(hit, count, slots)] = probe
        return count + jnp.where(hit, 1, 0)

    lax.fori_loop(0, probes, visit, 0, unroll=math.gcd(probes, 32))
    copies[1].wait()
    for slot in range(slots):
        probe = jnp.maximum(slot_ref[slot], 0)
        pick_ref[3 * slot] = slot_ref[slot]
        pick_ref[3 * slot + 1] = position_ref[0, probe]
        pick_ref[3 * slot + 2] = position_ref[1, probe]


def fetch_kernel(specimen_hbm, specimen_ref, sem):
    copy = pltpu.make_async_copy(specimen_hbm.at[0, :, :, 0 : specimen_ref.shape[2]], specimen_ref, sem)
    copy.start()
    copy.wait()


def place_kernel(pick_hbm, phase_hbm, table_hbm, weight_ref, right_ref, pick_ref, phase_ref, table_ref, sems):
    slots, length = right_ref.shape[0], right_ref.shape[2]
    beams, probes = phase_ref.shape
    half = length // 2
    cut = half + SPAN + 8
    pairs = [
        (pick_hbm, pick_ref),
        (phase_hbm, phase_ref),
        (table_hbm.at[0:cut], table_ref.at[0:cut]),
        (table_hbm.at[cut:], table_ref.at[cut:]),
    ]
    copies = [pltpu.make_async_copy(*pair, sems.at[index]) for index, pair in enumerate(pairs)]
    for copy in copies:
        copy.start()
    me = lax.axis_index("beam")
    lane = lax.broadcasted_iota(jnp.int32, (beams, probes), 1)
    row = lax.broadcasted_iota(jnp.int32, (beams, 128), 0)
    column = lax.broadcasted_iota(jnp.int32, (beams, 128), 1)
    flips = jnp.zeros_like(column)
    for step, mask in enumerate(partners(beams)):
        flips = flips ^ jnp.where((column >> step & 1) == 1, mask, 0)
    copies[0].wait()
    copies[1].wait()
    for slot in range(slots):
        pick = pick_ref[3 * slot]
        level = jnp.sum(jnp.where(lane == pick, phase_ref[...], 0), axis=1, keepdims=True)
        level = jnp.sum(jnp.where(row == flips ^ me, level, 0), axis=0, keepdims=True)
        level = jnp.sum(jnp.where(row == column, level, 0), axis=1, keepdims=True)
        level = jnp.broadcast_to(level, (beams, 128))
        scale = jnp.where(pick >= 0, 1.0 / math.sqrt(beams), 0.0)
        weight_ref[slot, 0] = cosine(level, LEVELS) * scale
        weight_ref[slot, 1] = cosine(level - LEVELS // 4, LEVELS) * scale
    for part in range(2):
        copies[2 + part].wait()
        rows = slice(part * half, (part + 1) * half)
        for slot in range(slots):
            cols = moved(table_ref, part * half + SPAN - pick_ref[3 * slot + 2], half)
            right_ref[slot, 0, rows], right_ref[slot, 1, rows] = split(cols)


def cosine(turns, length):
    quarter = length // 4
    shift = quarter.bit_length() - 1
    turns = turns & (length - 1)
    quadrant = (turns + quarter // 2) >> shift
    angle = (turns - (quadrant << shift)).astype(jnp.float32) * (two_pi / length)
    square = angle * angle
    even = 1.0 + square * (-1.0 / 2 + square * (1.0 / 24 + square * (-1.0 / 720 + square * (1.0 / 40320))))
    odd = angle * (1.0 + square * (-1.0 / 6 + square * (1.0 / 120 + square * (-1.0 / 5040))))
    value = jnp.where((quadrant & 1) == 0, even, odd)
    return jnp.where(((quadrant + 1) & 2) == 0, value, -value)


def probe_kernel(
    beam_ref,
    weight_ref,
    near_ref,
    right_ref,
    offset_ref,
    transmission_hbm,
    left_hbm,
    out_hbm,
    far_ref,
    left_ref,
    row_ref,
    col_ref,
    mix_ref,
    light_ref,
    lit_ref,
    half_refs,
    out_ref,
    start_ref,
    sems,
    out_sems,
):
    slots, length = out_ref.shape[0], transmission_hbm.shape[-1]
    beams = beam_ref.shape[0]
    depth = row_ref.shape[1]
    quarter = length // 4
    copy = pltpu.make_async_copy(offset_ref, start_ref, sems.at[0])
    copy.start()
    far = pltpu.make_async_copy(transmission_hbm.at[0, :, :, length // 2 :], far_ref, sems.at[2])
    far.start()
    left = pltpu.make_async_copy(left_hbm, left_ref, sems.at[1])
    left.start()
    row_freq = beam_ref[:, 0, 0:128]
    col_freq = beam_ref[:, 0, 128:256]
    lane = lax.broadcasted_iota(jnp.int32, (beams, depth), 1)
    member = lax.broadcasted_iota(jnp.int32, (beams, depth), 0)
    wide = jnp.concatenate([row_freq] * (depth // 128), axis=1)
    freq = jnp.sum(jnp.where(lane % beams == member, wide, 0), axis=0, keepdims=True)
    block = lax.broadcasted_iota(jnp.int32, (1, depth), 1) // beams
    shift = jnp.where(block % 2 == 1, quarter, 0)
    fine = lax.broadcasted_iota(jnp.int32, (STEP, depth), 0) * freq
    fine_cos, fine_sin = cosine(fine, length), cosine(fine - quarter, length)
    coarse = lax.broadcasted_iota(jnp.int32, (length // STEP, depth), 0) * (STEP * freq) - shift
    coarse_cos, coarse_sin = cosine(coarse, length), cosine(coarse - quarter, length)
    for index in range(length // STEP):
        waves = coarse_cos[index : index + 1] * fine_cos - coarse_sin[index : index + 1] * fine_sin
        high = waves.astype(jnp.bfloat16).astype(jnp.float32)
        parts = jnp.where(block < 4, high, jnp.where(block < 6, waves - high, 0.0))
        row_ref[index * STEP : (index + 1) * STEP] = parts.astype(jnp.bfloat16)
    pixel = lax.broadcasted_iota(jnp.int32, (beams, length), 1)
    turns = pixel * jnp.concatenate([col_freq] * (length // 128), axis=1)
    col_ref[0] = cosine(turns, length)
    col_ref[1] = cosine(turns - quarter, length)
    if depth > 6 * beams:
        for way in range(mix_ref.shape[0]):
            mix_ref[way, 6 * beams :] = jnp.zeros((depth - 6 * beams, 2 * length), jnp.bfloat16)

    def light(slot, way):
        weight_real = jnp.concatenate([weight_ref[slot, 0]] * (length // 128), axis=1)
        weight_imag = jnp.concatenate([weight_ref[slot, 1]] * (length // 128), axis=1)
        real = weight_real * col_ref[0] - weight_imag * col_ref[1]
        imag = weight_real * col_ref[1] + weight_imag * col_ref[0]
        tiles = [slice(start, start + 128) for start in range(0, length, 128)]
        for_cos = split(jnp.concatenate([x[:, tile] for tile in tiles for x in (real, imag)], axis=1))
        for_sin = split(jnp.concatenate([x[:, tile] for tile in tiles for x in (-imag, real)], axis=1))
        parts = [for_cos[0], for_sin[0], for_cos[1], for_sin[1], for_cos[0], for_sin[0]]
        for index, part in enumerate(parts):
            mix_ref[way, index * beams : (index + 1) * beams] = part

    def light_tile(tile, way):
        light_ref[way, tile] = dot(row_ref[...], mix_ref[way, :, tile * 256 : (tile + 1) * 256])

    def shine(tile, way):
        specimen_ref = near_ref if tile * 128 < length // 2 else far_ref
        cols = slice(tile * 128 % (length // 2), tile * 128 % (length // 2) + 128)
        stretch, start = tile * 128 // WIDE, tile * 128 % WIDE
        lanes = slice(start, start + 128)
        for row in range(0, length, 32):
            rows = slice(row, row + 32)
            light_real, light_imag = light_ref[way, tile, rows, 0:128], light_ref[way, tile, rows, 128:256]
            real, imag = specimen_ref[0, rows, cols], specimen_ref[1, rows, cols]
            high, low = split(real * light_real - imag * light_imag)
            lit_ref[way, stretch, 0, rows, lanes], lit_ref[way, stretch, 1, rows, lanes] = high, low
            high, low = split(real * light_imag + imag * light_real)
            lit_ref[way, length // WIDE + stretch, 0, rows, lanes], lit_ref[way, length // WIDE + stretch, 1, rows, lanes] = high, low

    def along_cols(slot, way):
        source, operator = [], []
        for stretch in range(2 * length // WIDE):
            rows = slice(stretch * WIDE % length, stretch * WIDE % length + WIDE)
            high, low = right_ref[slot, 0, rows], right_ref[slot, 1, rows]
            if stretch * WIDE >= length:
                high, low = (jnp.concatenate([-x[:, WINDOW:], x[:, :WINDOW]], axis=1) for x in (high, low))
            source += [lit_ref[way, stretch, 0], lit_ref[way, stretch, 0], lit_ref[way, stretch, 1]]
            operator += [high, low, high]
        half = dot(jnp.concatenate(source, axis=1), jnp.concatenate(operator, axis=0))
        half_refs[way][0:length] = half
        half_refs[way][length:] = half[0 : SPAN + 8]

    def along_rows(count):
        parts = []
        for slot in range(count):
            high, low = split(moved(half_refs[slot], start_ref[3 * slot + 1], length))
            parts.append(jnp.concatenate([high, low, high], axis=0))
        every = dot(left_ref[...], jnp.concatenate(parts, axis=1))
        for slot in range(count):
            full = every[:, 2 * slot * WINDOW : 2 * (slot + 1) * WINDOW]
            real = full[:WINDOW, :WINDOW] - full[WINDOW:, WINDOW:]
            imag = full[:WINDOW, WINDOW:] + full[WINDOW:, :WINDOW]
            out_ref[slot] = real * real + imag * imag

    def prepare(slot):
        light(slot, slot)
        light_tile(0, slot)
        for tile in range(1, length // 128):
            light_tile(tile, slot)
            if slot == 0 and tile == length // 256 + 1:
                far.wait()
            shine(tile - 1, slot)
        shine(length // 128 - 1, slot)

    def send(slot):
        pltpu.make_async_copy(out_ref.at[slot], out_hbm.at[slot], out_sems.at[slot]).start()

    def run(count):
        ready = 0
        for slot in range(count):
            wanted = min(slot + 2 if count == slots or slot else 1, count)
            for coming in range(ready, wanted):
                prepare(coming)
            ready = wanted
            along_cols(slot, slot)
        left.wait()
        along_rows(count)
        for slot in range(count, slots):
            out_ref[slot] = jnp.zeros((WINDOW, WINDOW), jnp.float32)

    copy.wait()
    full = start_ref[3 * slots - 3] >= 0
    pl.when(full)(lambda: run(slots))
    pl.when(jnp.logical_not(full))(lambda: run(slots - 1))
    for slot in range(slots):
        send(slot)
    for slot in range(slots):
        pltpu.make_async_copy(out_ref.at[slot], out_hbm.at[slot], out_sems.at[slot]).wait()


def probe_call(every, weight, specimen, right, offset, transmission, left):
    length = transmission.shape[-1]
    depth = pl.cdiv(6 * every.shape[0], 128) * 128
    weight, specimen, right = (pltpu.with_memory_space_constraint(x, pltpu.VMEM) for x in (weight, specimen, right))
    transmission, left = (pltpu.with_memory_space_constraint(x, pltpu.HBM) for x in (transmission, left))
    vmem = pl.BlockSpec(memory_space=pltpu.VMEM)
    anywhere = pl.BlockSpec(memory_space=pltpu.HBM)
    return pl.pallas_call(
        probe_kernel,
        out_shape=jax.ShapeDtypeStruct((CAP, WINDOW, WINDOW), jnp.float32),
        in_specs=[vmem] * 4 + [pl.BlockSpec(memory_space=pl.ANY)] + [anywhere] * 2,
        out_specs=anywhere,
        scratch_shapes=[
            pltpu.VMEM(specimen.shape, specimen.dtype),
            pltpu.VMEM(left.shape, left.dtype),
            pltpu.VMEM((length, depth), jnp.bfloat16),
            pltpu.VMEM((2, every.shape[0], length), jnp.float32),
            pltpu.VMEM((CAP, depth, 2 * length), jnp.bfloat16),
            pltpu.VMEM((CAP, length // 128, length, 256), jnp.float32),
            pltpu.VMEM((CAP, 2 * length // WIDE, 2, length, WIDE), jnp.bfloat16),
            [pltpu.VMEM((length + SPAN + 8, 2 * WINDOW), jnp.float32) for _ in range(CAP)],
            pltpu.VMEM((CAP, WINDOW, WINDOW), jnp.float32),
            pltpu.SMEM((3 * CAP,), jnp.int32),
            pltpu.SemaphoreType.DMA((3,)),
            pltpu.SemaphoreType.DMA((CAP,)),
        ],
        compiler_params=pltpu.CompilerParams(vmem_limit_bytes=VMEM_LIMIT),
        name="probes",
    )(every, weight, specimen, right, offset, transmission, left)


def local(transmission, beams, phases, positions, owner):
    length = transmission.shape[-1]
    beam_count = lax.axis_size("beam")
    beam_total = phases.shape[1]
    every = jnp.broadcast_to(beams[:, :, None], (1, 2, 128)).reshape(1, 1, 256)
    for mask in partners(beam_count):
        pairs = [(here, here ^ mask) for here in range(beam_count)]
        other = lax.ppermute(every, "beam", pairs)
        every = jnp.concatenate([every, other], axis=0)
    vmem = pl.BlockSpec(memory_space=pltpu.VMEM)
    smem = pl.BlockSpec(memory_space=pltpu.SMEM)
    anywhere = pl.BlockSpec(memory_space=pltpu.HBM)
    params = pltpu.CompilerParams(vmem_limit_bytes=VMEM_LIMIT)
    pick = pl.pallas_call(
        pick_kernel,
        out_shape=jax.ShapeDtypeStruct((3 * CAP,), jnp.int32),
        in_specs=[anywhere] * 2,
        out_specs=smem,
        scratch_shapes=[
            pltpu.SMEM(owner.shape, jnp.int32),
            pltpu.SMEM(positions.shape[::-1], jnp.int32),
            pltpu.SMEM((CAP + 1,), jnp.int32),
            pltpu.SemaphoreType.DMA((2,)),
        ],
        compiler_params=params,
        name="pick",
    )(*(pltpu.with_memory_space_constraint(x, pltpu.HBM) for x in (owner, positions.T)))
    specimen = pl.pallas_call(
        fetch_kernel,
        out_shape=pltpu.VMEM((2, length, length // 2), jnp.float32),
        in_specs=[anywhere],
        out_specs=vmem,
        scratch_shapes=[pltpu.SemaphoreType.DMA],
        compiler_params=params,
        name="fetch",
    )(pltpu.with_memory_space_constraint(transmission, pltpu.HBM))
    table = window_operator(length)
    weight, right = pl.pallas_call(
        place_kernel,
        out_shape=(
            pltpu.VMEM((CAP, 2, beam_total, 128), jnp.float32),
            pltpu.VMEM((CAP, 2, length, 2 * WINDOW), jnp.bfloat16),
        ),
        in_specs=[pl.BlockSpec(memory_space=pl.ANY), anywhere, anywhere],
        out_specs=(vmem, vmem),
        scratch_shapes=[
            pltpu.SMEM((3 * CAP,), jnp.int32),
            pltpu.VMEM(phases.shape[::-1], jnp.int32),
            pltpu.VMEM(table.shape, jnp.float32),
            pltpu.SemaphoreType.DMA((4,)),
        ],
        compiler_params=params,
        name="place",
    )(pick, *(pltpu.with_memory_space_constraint(x, pltpu.HBM) for x in (phases.T, jnp.asarray(table))))
    return probe_call(every, weight, specimen, right, pick, transmission, jnp.asarray(row_operator(table)))


def solution(mesh):
    in_specs = (P("groups", None, None, None), P("beam", None), P(), P(), P())
    out_specs = P(("groups", "beam"), None, None)
    return jax.shard_map(local, mesh=mesh, in_specs=in_specs, out_specs=out_specs, check_vma=False)
```
